128 devices in a mesh: req: 32 (over x, z, core), mlp: 4 (over y).
Axes of the slice: x: 4, y: 4, z: 4, core: 2. Of those that a mesh axis runs over, the one named last changes fastest.
Arguments:
- queries: bfloat16 [16896, 2048], P('req', 'mlp'), may hold values from -6 to 6
- key_cache: bfloat16 [2560, 128, 1024], P('req', None, 'mlp'), may hold values from -6 to 6
- value_cache: bfloat16 [2560, 128, 1024], P('req', None, 'mlp'), may hold values from -6 to 6
- decode_len: int32 [512], P('req'), may hold values from 1 to 4096, as said below
- stretch_start: int32 [32], P('req'), may hold values from 0 to 3584, as said below
- page_table: int32 [544, 32], P('req'), may hold values from 0 to 79, as said below
- hidden_in: bfloat16 [16896, 2304], P('req')
- o_weight: bfloat16 [2048, 2304], P('mlp'), may hold values from -0.125 to 0.125
- attn_gain: float32 [2304], replicated, may hold values from 0.1 to 1.9
- ffn_in_gain: float32 [2304], replicated, may hold values from 0.1 to 1.9
- ffn_out_gain: float32 [2304], replicated, may hold values from 0.1 to 1.9
- w_gate: bfloat16 [2304, 9216], P('req', 'mlp'), may hold values from -0.125 to 0.125
- w_up: bfloat16 [2304, 9216], P('req', 'mlp'), may hold values from -0.125 to 0.125
- w_down: bfloat16 [2304, 9216], P('req', 'mlp')
Outputs:
- layer_out: bfloat16 [16896, 2304], P('req', 'mlp')
The draws below stay inside these ranges and needn't reach their ends.
Inputs may be any that keep to these rules, and one draw needn't show every extreme that they name: `decode_len`: each decode request's tokens fill its first pages; request 1 of req index 1 holds 4096 tokens. `stretch_start`: req index 0 starts at 3584, req index 1 at 0. `page_table`: row j of req index r's block of 17 rows names request j's pages by slot in that index's own pool of 80 pages; the slots holding a req index's tokens are all distinct; entries past a request's last page are valid slots that hold none of its tokens.
All inputs are finite; a program needn't handle non-finite values.
Results may differ from the reference program's by a relative error of at most 0.014.
Values may be sent and summed in bfloat16 or wider, within the bound.
A program may use at most 128 MiB of HBM per device.

```python
import jax
import jax.numpy as jnp
from jax import lax

D = 2304
H = 8
KVH = 4
HD = 256
FF = 9216
PAGE = 128
MAXP = 32
PRE_DEV = 512
DEC_DEV = 16
MAXLEN = 4096
REQ_DEV = 17
POOL_DEV = 80
ROWS_DEV = 528
ROWS = 16896
REQS = 544
DECS = 512
POOL = 2560
N_REQ = 32


def layout_draw(key):
    keys = jax.random.split(jax.random.fold_in(key, 7), N_REQ)

    def one_index(sub, index):
        k_start, k_share, k_weight, k_tail, k_perm = jax.random.split(sub, 5)
        start = jax.random.randint(k_start, (), 0, MAXLEN - PRE_DEV + 1, dtype=jnp.int32)
        start = jnp.where(index == 0, MAXLEN - PRE_DEV, jnp.where(index == 1, 0, start))
        first = (start + PRE_DEV + PAGE - 1) // PAGE
        avail = POOL_DEV - first - DEC_DEV
        share = jax.random.randint(k_share, (), 1, 9, dtype=jnp.int32)
        share = jnp.where(index == 1, 0, share)
        budget = avail * share // 8
        powers = jax.random.randint(k_weight, (DEC_DEV,), 0, 6, dtype=jnp.int32)
        weights = jnp.left_shift(jnp.ones((DEC_DEV,), jnp.int32), powers)
        extra = jnp.minimum(budget * weights // jnp.sum(weights), MAXP - 1)
        slot_ids = jnp.arange(DEC_DEV, dtype=jnp.int32)
        longest = (index == 1) & (slot_ids == 0)
        pages = jnp.where(longest, MAXP, 1 + extra)
        tail = jax.random.randint(k_tail, (DEC_DEV,), 1, PAGE + 1, dtype=jnp.int32)
        lengths = jnp.where(longest, MAXLEN, (pages - 1) * PAGE + tail)
        counts = jnp.concatenate([first[None], pages])
        offsets = jnp.cumsum(counts) - counts
        perm = jax.random.permutation(k_perm, POOL_DEV).astype(jnp.int32)
        entries = (offsets[:, None] + jnp.arange(MAXP, dtype=jnp.int32)[None, :]) % POOL_DEV
        return (start, lengths, perm[entries])
    starts, lengths, tables = jax.vmap(one_index)(keys, jnp.arange(N_REQ, dtype=jnp.int32))
    return (starts.astype(jnp.int32), lengths.reshape(DECS).astype(jnp.int32), tables.reshape(REQS, MAXP).astype(jnp.int32))


def draw_decode_len(key, part):
    return layout_draw(key)[1]


def draw_stretch_start(key, part):
    return layout_draw(key)[0]


def draw_page_table(key, part):
    return layout_draw(key)[2]


def shared_signs(key):
    picks = jax.random.randint(jax.random.fold_in(key, 23), (KVH, HD), 0, 2, dtype=jnp.int32)
    return 2.0 * picks.astype(jnp.float32) - 1.0


def draw_queries(key, part):
    k_base, k_amp = jax.random.split(jax.random.fold_in(key, 29), 2)
    signs = jnp.repeat(shared_signs(key), H // KVH, axis=0)
    base = jax.random.normal(k_base, (ROWS, H, HD), jnp.float32)
    amp = jax.random.uniform(k_amp, (ROWS, H, 1), jnp.float32, 0.0, 2.5)
    values = jnp.clip(base + amp * signs[None, :, :], -6.0, 6.0)
    return values.reshape(ROWS, H * HD).astype(jnp.bfloat16)


def draw_key_cache(key, part):
    k_base, k_amp = jax.random.split(jax.random.fold_in(key, 31), 2)
    signs = shared_signs(key)
    base = jax.random.normal(k_base, (POOL, PAGE, KVH, HD), jnp.float32)
    amp = jax.random.uniform(k_amp, (POOL, PAGE, KVH, 1), jnp.float32, -2.0, 2.0)
    values = jnp.clip(base + amp * signs[None, None, :, :], -6.0, 6.0)
    return values.reshape(POOL, PAGE, KVH * HD).astype(jnp.bfloat16)


def draw_hidden_in(key, part):
    k_base, k_rows, k_cols = jax.random.split(jax.random.fold_in(key, 11), 3)
    rising = 3.0 ** (jnp.arange(D, dtype=jnp.float32) / D - 0.5)
    base = jax.random.normal(k_base, (ROWS, D), jnp.float32)
    rows = jnp.exp(jax.random.uniform(k_rows, (ROWS, 1), jnp.float32, -0.4, 0.4))
    cols = jnp.exp(jax.random.uniform(k_cols, (1, D), jnp.float32, -0.4, 0.4))
    return (base * rows * cols * rising[None, :]).astype(jnp.bfloat16)


def draw_w_down(key, part):
    k_base, k_rows = jax.random.split(jax.random.fold_in(key, 13), 2)
    rising = 3.0 ** (jnp.arange(D, dtype=jnp.float32) / D - 0.5)
    base = jax.random.normal(k_base, (D, FF), jnp.float32)
    rows = jnp.exp(jax.random.uniform(k_rows, (D, 1), jnp.float32, -0.4, 0.4))
    return (base * rows * rising[:, None] * FF ** (-0.5)).astype(jnp.bfloat16)


def shard_levels(key, dims, shards, smallest, high):
    level = 1.0
    for dim, shards_of in shards:
        draws = jax.random.uniform(jax.random.fold_in(jax.random.fold_in(key, 6), dim), (shards_of,), jnp.float32, smallest / len(shards), high / len(shards))
        level = level * jnp.repeat(jnp.exp(draws), dims[dim] // shards_of).reshape((-1,) + (1,) * (len(dims) - 1 - dim))
    return level


def scatter_about(stream_key, dims, scale, bound, cuts=(), kind=jnp.bfloat16):
    values = scale * jax.random.normal(stream_key, dims, jnp.float32)
    if cuts:
        values = values * shard_levels(stream_key, dims, cuts, -0.22, 0.18)
    return jnp.clip(values, -bound, bound).astype(kind)


def setup_inputs(seed: int = 0) -> dict:
    splits = jax.random.split(jax.random.key(seed), 15)
    return {
        "queries": draw_queries(jax.random.fold_in(splits[14], 71), 0),
        "key_cache": draw_key_cache(jax.random.fold_in(splits[14], 71), 0),
        "value_cache": scatter_about(splits[2], (POOL, PAGE, KVH * HD), 1.0, 6.0, ((0, 32), (2, 4))),
        "decode_len": draw_decode_len(jax.random.fold_in(splits[14], 71), 0),
        "stretch_start": draw_stretch_start(jax.random.fold_in(splits[14], 71), 0),
        "page_table": draw_page_table(jax.random.fold_in(splits[14], 71), 0),
        "hidden_in": draw_hidden_in(jax.random.fold_in(splits[14], 71), 0),
        "o_weight": scatter_about(splits[7], (H * HD, D), (H * HD) ** -0.5, 0.125, ((0, 4),)),
        "attn_gain": jnp.clip(1.0 + 0.18 * jax.random.normal(splits[8], (D,), jnp.float32), 0.1, 1.9),
        "ffn_in_gain": jnp.clip(1.0 + 0.18 * jax.random.normal(splits[9], (D,), jnp.float32), 0.1, 1.9),
        "ffn_out_gain": jnp.clip(1.0 + 0.18 * jax.random.normal(splits[10], (D,), jnp.float32), 0.1, 1.9),
        "w_gate": scatter_about(splits[11], (D, FF), D ** -0.5, 0.125, ((0, 32), (1, 4))),
        "w_up": scatter_about(splits[12], (D, FF), D ** -0.5, 0.125, ((0, 32), (1, 4))),
        "w_down": draw_w_down(jax.random.fold_in(splits[14], 71), 0),
    }


EPS = 1e-06
CAP = 50.0

def rms(values, gain):
    return values * lax.rsqrt(lax.optimization_barrier(jnp.mean(values * values, axis=-1, keepdims=True)) + EPS) * gain

def attend_index(args):
    query, keys, values, table, lengths, start = args
    rep = H // KVH
    keys_req = keys[table].reshape(REQ_DEV, MAXLEN, KVH, HD).astype(jnp.float32)
    vals_req = values[table].reshape(REQ_DEV, MAXLEN, KVH, HD).astype(jnp.float32)
    query = query.reshape(ROWS_DEV, KVH, rep, HD).astype(jnp.float32)
    position = jnp.arange(MAXLEN, dtype=jnp.int32)

    def finish(scores, mask, vals, form):
        capped = CAP * jnp.tanh(scores / (16.0 * CAP))
        weight = jnp.where(mask, jnp.exp(capped), jnp.float32(0.0))
        denom = lax.optimization_barrier(jnp.sum(weight, axis=-1))
        rounded = lax.optimization_barrier(weight.astype(jnp.bfloat16)).astype(jnp.float32)
        numer = jnp.einsum(form, rounded, vals)
        return (numer / denom[..., None]).astype(jnp.bfloat16)
    pre_q = query[:PRE_DEV]
    pre_scores = jnp.einsum('rghd,tgd->rght', pre_q, keys_req[0])
    limit = start + jnp.arange(PRE_DEV, dtype=jnp.int32) + 1
    pre_mask = position[None, None, None, :] < limit[:, None, None, None]
    pre_out = finish(pre_scores, pre_mask, vals_req[0], 'rght,tgd->rghd')
    dec_q = query[PRE_DEV:]
    dec_scores = jnp.einsum('rghd,rtgd->rght', dec_q, keys_req[1:])
    dec_mask = position[None, None, None, :] < lengths[:, None, None, None]
    dec_out = finish(dec_scores, dec_mask, vals_req[1:], 'rght,rtgd->rghd')
    return jnp.concatenate([pre_out, dec_out], axis=0).reshape(ROWS_DEV, H * HD)

def reference(queries, key_cache, value_cache, decode_len, stretch_start, page_table, hidden_in, o_weight, attn_gain, ffn_in_gain, ffn_out_gain, w_gate, w_up, w_down):
    groups = (queries.reshape(N_REQ, ROWS_DEV, H * HD), key_cache.reshape(N_REQ, POOL_DEV, PAGE, KVH * HD), value_cache.reshape(N_REQ, POOL_DEV, PAGE, KVH * HD), page_table.reshape(N_REQ, REQ_DEV, MAXP).astype(jnp.int32), decode_len.reshape(N_REQ, DEC_DEV).astype(jnp.int32), stretch_start.astype(jnp.int32))
    attended = lax.map(attend_index, groups).reshape(ROWS, H * HD)
    projected = jnp.dot(attended, o_weight, preferred_element_type=jnp.float32)
    resid = hidden_in.astype(jnp.float32) + rms(projected, attn_gain)
    normed = rms(resid, ffn_in_gain).astype(jnp.bfloat16)
    gate = jnp.dot(normed, w_gate, preferred_element_type=jnp.float32)
    up_part = jnp.dot(normed, w_up, preferred_element_type=jnp.float32)
    act = (jax.nn.gelu(gate, approximate=True) * up_part).astype(jnp.bfloat16)
    ffn = jnp.dot(act, w_down.T, preferred_element_type=jnp.float32)
    return (resid + rms(ffn, ffn_out_gain)).astype(jnp.bfloat16)
```

```python
import math

import jax
import jax.numpy as jnp
from jax import lax
from jax.sharding import PartitionSpec as P

H = 8
KVH = 4
HD = 256
PRE_DEV = 512
DEC_DEV = 16


EPS = 1e-06
CAP = 50.0


def rms(values, gain):
    return values * lax.rsqrt(jnp.mean(values * values, axis=-1, keepdims=True) + EPS) * gain


def capped_weight(scores, visible):
    capped = CAP * jnp.tanh(scores / (16.0 * CAP))
    return jnp.where(visible, jnp.exp(capped), jnp.float32(0.0))


def attend(queries, key_cache, value_cache, decode_len, stretch_start, page_table):
    rows = queries.shape[0]
    local_kv = key_cache.shape[2] // HD
    rep = H // KVH
    pool = key_cache.shape[0]
    page_len = key_cache.shape[1]
    max_pages = page_table.shape[1]
    query = queries.reshape(rows, local_kv, rep, HD)
    pre_q = query[:PRE_DEV]
    dec_q = query[PRE_DEV:]
    start = stretch_start[0]

    pre_keys = key_cache[page_table[0]].reshape(max_pages * page_len, local_kv, HD)
    pre_vals = value_cache[page_table[0]].reshape(max_pages * page_len, local_kv, HD)
    position = jnp.arange(max_pages * page_len, dtype=jnp.int32)
    limit = start + jnp.arange(PRE_DEV, dtype=jnp.int32) + 1
    pre_scores = jnp.einsum(
        "rghd,tgd->rght", pre_q, pre_keys, preferred_element_type=jnp.float32
    )
    pre_weight = capped_weight(
        pre_scores, position[None, None, None, :] < limit[:, None, None, None]
    )
    pre_num = jnp.einsum(
        "rght,tgd->rghd",
        pre_weight.astype(jnp.bfloat16),
        pre_vals,
        preferred_element_type=jnp.float32,
    )
    pre_den = jnp.sum(pre_weight, axis=-1)

    table = page_table[1:]
    page_idx = jnp.arange(max_pages, dtype=jnp.int32)
    used = page_idx[None, :] * page_len < decode_len[:, None]
    owned = (table[:, :, None] == jnp.arange(pool, dtype=jnp.int32)[None, None, :]) & used[
        :, :, None
    ]
    base = jnp.min(
        jnp.where(owned, page_idx[None, :, None] * page_len, jnp.int32(1 << 30)), axis=1
    )
    dec_pos = (base[:, :, None] + jnp.arange(page_len, dtype=jnp.int32)[None, None, :]).reshape(
        DEC_DEV, pool * page_len
    )
    all_keys = key_cache.reshape(pool * page_len, local_kv, HD)
    all_vals = value_cache.reshape(pool * page_len, local_kv, HD)
    dec_scores = jnp.einsum(
        "rghd,tgd->rght", dec_q, all_keys, preferred_element_type=jnp.float32
    )
    dec_weight = capped_weight(dec_scores, (dec_pos < decode_len[:, None])[:, None, None, :])
    dec_num = jnp.einsum(
        "rght,tgd->rghd",
        dec_weight.astype(jnp.bfloat16),
        all_vals,
        preferred_element_type=jnp.float32,
    )
    dec_den = jnp.sum(dec_weight, axis=-1)

    pre_out = (pre_num / pre_den[..., None]).astype(jnp.bfloat16)
    dec_out = (dec_num / dec_den[..., None]).astype(jnp.bfloat16)
    return jnp.concatenate([pre_out, dec_out], axis=0).reshape(rows, local_kv * rep * HD)


def per_device(
    queries,
    key_cache,
    value_cache,
    decode_len,
    stretch_start,
    page_table,
    hidden_in,
    o_weight,
    attn_gain,
    ffn_in_gain,
    ffn_out_gain,
    w_gate,
    w_up,
    w_down,
):
    attended = attend(queries, key_cache, value_cache, decode_len, stretch_start, page_table)
    projected = lax.psum(
        jnp.dot(attended, o_weight, preferred_element_type=jnp.float32).astype(jnp.bfloat16), "mlp"
    ).astype(jnp.float32)
    resid = hidden_in.astype(jnp.float32) + rms(projected, attn_gain)
    normed = rms(resid, ffn_in_gain).astype(jnp.bfloat16)
    gate = jnp.dot(
        normed,
        lax.all_gather(w_gate, "req", axis=0, tiled=True),
        preferred_element_type=jnp.float32,
    )
    up_part = jnp.dot(
        normed, lax.all_gather(w_up, "req", axis=0, tiled=True), preferred_element_type=jnp.float32
    )
    act = (jax.nn.gelu(gate, approximate=True) * up_part).astype(jnp.bfloat16)
    partial_out = lax.dot_general(
        act,
        lax.all_gather(w_down, "req", axis=0, tiled=True),
        (((1,), (1,)), ((), ())),
        preferred_element_type=jnp.float32,
    )
    width = hidden_in.shape[1] // lax.axis_size("mlp")
    first = lax.axis_index("mlp") * width
    total = lax.psum(partial_out.astype(jnp.bfloat16), "mlp").astype(jnp.float32)
    combined = resid + rms(total, ffn_out_gain)
    result = lax.dynamic_slice_in_dim(combined, first, width, 1)
    return result.astype(jnp.bfloat16)


def solution(mesh):
    return jax.shard_map(
        per_device,
        mesh=mesh,
        in_specs=(
            P("req", "mlp"),
            P("req", None, "mlp"),
            P("req", None, "mlp"),
            P("req"),
            P("req"),
            P("req", None),
            P("req", None),
            P("mlp", None),
            P(),
            P(),
            P(),
            P("req", "mlp"),
            P("req", "mlp"),
            P("req", "mlp"),
        ),
        out_specs=P("req", "mlp"),
        check_vma=False,
    )
```

```python
import jax
import jax.numpy as jnp
from jax import lax
from jax.sharding import PartitionSpec as P

H = 8
KVH = 4
HD = 256
PRE_DEV = 512
DEC_DEV = 16


EPS = 1e-06
CAP = 50.0


def rms(values, gain):
    return values * lax.rsqrt(jnp.mean(values * values, axis=-1, keepdims=True) + EPS) * gain


def capped_weight(scores, visible):
    capped = CAP * jnp.tanh(scores / (16.0 * CAP))
    return jnp.where(visible, jnp.exp(capped), jnp.float32(0.0))


def attend(queries, key_cache, value_cache, decode_len, stretch_start, page_table):
    rows = queries.shape[0]
    local_kv = key_cache.shape[2] // HD
    rep = H // KVH
    pool = key_cache.shape[0]
    page_len = key_cache.shape[1]
    max_pages = page_table.shape[1]
    query = queries.reshape(rows, local_kv, rep, HD)
    pre_q = query[:PRE_DEV]
    dec_q = query[PRE_DEV:]
    start = stretch_start[0]

    pre_keys = key_cache[page_table[0]].reshape(max_pages * page_len, local_kv, HD)
    pre_vals = value_cache[page_table[0]].reshape(max_pages * page_len, local_kv, HD)
    position = jnp.arange(max_pages * page_len, dtype=jnp.int32)
    limit = start + jnp.arange(PRE_DEV, dtype=jnp.int32) + 1
    pre_scores = jnp.einsum("rghd,tgd->rght", pre_q, pre_keys, preferred_element_type=jnp.float32)
    pre_weight = capped_weight(
        pre_scores, position[None, None, None, :] < limit[:, None, None, None]
    )
    pre_num = jnp.einsum(
        "rght,tgd->rghd",
        pre_weight.astype(jnp.bfloat16),
        pre_vals,
        preferred_element_type=jnp.float32,
    )
    pre_den = jnp.sum(pre_weight, axis=-1)

    table = page_table[1:]
    page_idx = jnp.arange(max_pages, dtype=jnp.int32)
    used = page_idx[None, :] * page_len < decode_len[:, None]
    owned = (table[:, :, None] == jnp.arange(pool, dtype=jnp.int32)[None, None, :]) & used[
        :, :, None
    ]
    base = jnp.min(
        jnp.where(owned, page_idx[None, :, None] * page_len, jnp.int32(1 << 30)), axis=1
    )
    dec_pos = (base[:, :, None] + jnp.arange(page_len, dtype=jnp.int32)[None, None, :]).reshape(
        DEC_DEV, pool * page_len
    )
    all_keys = key_cache.reshape(pool * page_len, local_kv, HD)
    all_vals = value_cache.reshape(pool * page_len, local_kv, HD)
    dec_scores = jnp.einsum(
        "rghd,tgd->rght", dec_q, all_keys, preferred_element_type=jnp.float32
    )
    dec_weight = capped_weight(dec_scores, (dec_pos < decode_len[:, None])[:, None, None, :])
    dec_num = jnp.einsum(
        "rght,tgd->rghd",
        dec_weight.astype(jnp.bfloat16),
        all_vals,
        preferred_element_type=jnp.float32,
    )
    dec_den = jnp.sum(dec_weight, axis=-1)

    pre_out = (pre_num / pre_den[..., None]).astype(jnp.bfloat16)
    dec_out = (dec_num / dec_den[..., None]).astype(jnp.bfloat16)
    return jnp.concatenate([pre_out, dec_out], axis=0).reshape(rows, local_kv * rep * HD)


def split_weight(weight):
    return lax.all_to_all(weight, "core", 1, 0, tiled=True)


def per_device(
    queries,
    key_cache,
    value_cache,
    decode_len,
    stretch_start,
    page_table,
    hidden_in,
    o_weight,
    attn_gain,
    ffn_in_gain,
    ffn_out_gain,
    w_gate,
    w_up,
    w_down,
):
    gate_w = split_weight(w_gate)
    up_w = split_weight(w_up)
    down_w = split_weight(w_down)
    queries, gate_w, up_w, down_w = lax.optimization_barrier((queries, gate_w, up_w, down_w))
    gate_w = lax.all_gather(gate_w, "chip", axis=0, tiled=True)
    up_w = lax.all_gather(up_w, "chip", axis=0, tiled=True)
    down_w = lax.all_gather(down_w, "chip", axis=0, tiled=True)
    attended = attend(queries, key_cache, value_cache, decode_len, stretch_start, page_table)
    projected = lax.psum(
        jnp.dot(attended, o_weight, preferred_element_type=jnp.float32).astype(jnp.bfloat16), "mlp"
    ).astype(jnp.float32)
    projected, gate_w, up_w, down_w = lax.optimization_barrier((projected, gate_w, up_w, down_w))
    resid = hidden_in.astype(jnp.float32) + rms(projected, attn_gain)
    normed = rms(resid, ffn_in_gain).astype(jnp.bfloat16)
    pair = lax.all_gather(normed, "core", axis=0, tiled=True)
    gate = jnp.dot(pair, gate_w, preferred_element_type=jnp.float32)
    up_part = jnp.dot(pair, up_w, preferred_element_type=jnp.float32)
    act = (jax.nn.gelu(gate, approximate=True) * up_part).astype(jnp.bfloat16)
    partial_out = lax.dot_general(
        act, down_w, (((1,), (1,)), ((), ())), preferred_element_type=jnp.float32
    )
    rows_part = lax.psum_scatter(
        partial_out.astype(jnp.bfloat16), "core", scatter_dimension=0, tiled=True
    )
    total = lax.psum_scatter(rows_part, "mlp", scatter_dimension=1, tiled=True).astype(
        jnp.float32
    )
    width = total.shape[1]
    first = lax.axis_index("mlp") * width
    square = lax.psum(jnp.sum(total * total, axis=-1, keepdims=True), "mlp")
    scale = lax.rsqrt(square / hidden_in.shape[1] + EPS)
    gain = lax.dynamic_slice_in_dim(ffn_out_gain, first, width, 0)
    kept = lax.dynamic_slice_in_dim(resid, first, width, 1)
    return (kept + total * scale * gain).astype(jnp.bfloat16)


def solution(mesh):
    devices = mesh.devices
    chips = devices.shape[0] // 2
    split = jax.sharding.Mesh(
        devices.reshape(chips, 2, devices.shape[1]), ("chip", "core", "mlp")
    )
    req = ("chip", "core")
    return jax.shard_map(
        per_device,
        mesh=split,
        in_specs=(
            P(req, "mlp"),
            P(req, None, "mlp"),
            P(req, None, "mlp"),
            P(req),
            P(req),
            P(req, None),
            P(req, None),
            P("mlp", None),
            P(),
            P(),
            P(),
            P(req, "mlp"),
            P(req, "mlp"),
            P(req, "mlp"),
        ),
        out_specs=P(req, "mlp"),
        check_vma=False,
    )
```

```python
import math

import jax
import jax.numpy as jnp
from jax import lax
from jax.sharding import PartitionSpec as P

H = 8
KVH = 4
HD = 256
PRE_DEV = 512
DEC_DEV = 16


EPS = 1e-06
CAP = 50.0


def rms(values, gain):
    return values * lax.rsqrt(jnp.mean(values * values, axis=-1, keepdims=True) + EPS) * gain


def capped_weight(scores, visible):
    capped = CAP * jnp.tanh(scores / (16.0 * CAP))
    return jnp.where(visible, jnp.exp(capped), jnp.float32(0.0))


def attend(queries, key_cache, value_cache, decode_len, stretch_start, page_table):
    rows = queries.shape[0]
    local_kv = key_cache.shape[2] // HD
    rep = H // KVH
    pool = key_cache.shape[0]
    page_len = key_cache.shape[1]
    max_pages = page_table.shape[1]
    query = queries.reshape(rows, local_kv, rep, HD)
    pre_q = query[:PRE_DEV]
    dec_q = query[PRE_DEV:]
    start = stretch_start[0]

    pre_keys = key_cache[page_table[0]].reshape(max_pages * page_len, local_kv, HD)
    pre_vals = value_cache[page_table[0]].reshape(max_pages * page_len, local_kv, HD)
    position = jnp.arange(max_pages * page_len, dtype=jnp.int32)
    limit = start + jnp.arange(PRE_DEV, dtype=jnp.int32) + 1
    pre_scores = jnp.einsum(
        "rghd,tgd->rght", pre_q, pre_keys, preferred_element_type=jnp.float32
    )
    pre_weight = capped_weight(
        pre_scores, position[None, None, None, :] < limit[:, None, None, None]
    )
    pre_num = jnp.einsum(
        "rght,tgd->rghd",
        pre_weight.astype(jnp.bfloat16),
        pre_vals,
        preferred_element_type=jnp.float32,
    )
    pre_den = jnp.sum(pre_weight, axis=-1)

    table = page_table[1:]
    page_idx = jnp.arange(max_pages, dtype=jnp.int32)
    used = page_idx[None, :] * page_len < decode_len[:, None]
    owned = (table[:, :, None] == jnp.arange(pool, dtype=jnp.int32)[None, None, :]) & used[
        :, :, None
    ]
    base = jnp.min(
        jnp.where(owned, page_idx[None, :, None] * page_len, jnp.int32(1 << 30)), axis=1
    )
    dec_pos = (base[:, :, None] + jnp.arange(page_len, dtype=jnp.int32)[None, None, :]).reshape(
        DEC_DEV, pool * page_len
    )
    all_keys = key_cache.reshape(pool * page_len, local_kv, HD)
    all_vals = value_cache.reshape(pool * page_len, local_kv, HD)
    dec_scores = jnp.einsum(
        "rghd,tgd->rght", dec_q, all_keys, preferred_element_type=jnp.float32
    )
    dec_weight = capped_weight(dec_scores, (dec_pos < decode_len[:, None])[:, None, None, :])
    dec_num = jnp.einsum(
        "rght,tgd->rghd",
        dec_weight.astype(jnp.bfloat16),
        all_vals,
        preferred_element_type=jnp.float32,
    )
    dec_den = jnp.sum(dec_weight, axis=-1)

    pre_out = (pre_num / pre_den[..., None]).astype(jnp.bfloat16)
    dec_out = (dec_num / dec_den[..., None]).astype(jnp.bfloat16)
    return jnp.concatenate([pre_out, dec_out], axis=0).reshape(rows, local_kv * rep * HD)


def per_device(
    queries,
    key_cache,
    value_cache,
    decode_len,
    stretch_start,
    page_table,
    hidden_in,
    o_weight,
    attn_gain,
    ffn_in_gain,
    ffn_out_gain,
    w_gate,
    w_up,
    w_down,
):
    weights = lax.all_gather(
        jnp.stack([w_gate, w_up, w_down]), "req", axis=1, tiled=True
    )
    attended = attend(queries, key_cache, value_cache, decode_len, stretch_start, page_table)
    projected = lax.psum(
        jnp.dot(attended, o_weight, preferred_element_type=jnp.float32).astype(jnp.bfloat16), "mlp"
    ).astype(jnp.float32)
    resid = hidden_in.astype(jnp.float32) + rms(projected, attn_gain)
    normed = rms(resid, ffn_in_gain).astype(jnp.bfloat16)
    gate = jnp.dot(normed, weights[0], preferred_element_type=jnp.float32)
    up_part = jnp.dot(normed, weights[1], preferred_element_type=jnp.float32)
    act = (jax.nn.gelu(gate, approximate=True) * up_part).astype(jnp.bfloat16)
    partial_out = lax.dot_general(
        act, weights[2], (((1,), (1,)), ((), ())), preferred_element_type=jnp.float32
    )
    total = lax.psum_scatter(
        partial_out.astype(jnp.bfloat16), "mlp", scatter_dimension=1, tiled=True
    ).astype(jnp.float32)
    width = total.shape[1]
    first = lax.axis_index("mlp") * width
    square = lax.psum(jnp.sum(total * total, axis=-1, keepdims=True), "mlp")
    scale = lax.rsqrt(square / hidden_in.shape[1] + EPS)
    gain = lax.dynamic_slice_in_dim(ffn_out_gain, first, width, 0)
    kept = lax.dynamic_slice_in_dim(resid, first, width, 1)
    return (kept + total * scale * gain).astype(jnp.bfloat16)


def solution(mesh):
    return jax.shard_map(
        per_device,
        mesh=mesh,
        in_specs=(
            P("req", "mlp"),
            P("req", None, "mlp"),
            P("req", None, "mlp"),
            P("req"),
            P("req"),
            P("req", None),
            P("req", None),
            P("mlp", None),
            P(),
            P(),
            P(),
            P("req", "mlp"),
            P("req", "mlp"),
            P("req", "mlp"),
        ),
        out_specs=P("req", "mlp"),
        check_vma=False,
    )
```

```python
import jax
import jax.numpy as jnp
from jax import lax
from jax.sharding import PartitionSpec as P


H = 8
KVH = 4
HD = 256
PRE_DEV = 512
DEC_DEV = 16


EPS = 1e-06
CAP = 50.0


def rms(values, gain):
    return values * lax.rsqrt(jnp.mean(values * values, axis=-1, keepdims=True) + EPS) * gain


def capped_weight(scores, visible):
    capped = CAP * jnp.tanh(scores / (16.0 * CAP))
    return jnp.where(visible, jnp.exp(capped), jnp.float32(0.0))


def attend(queries, key_cache, value_cache, decode_len, stretch_start, page_table):
    rows = queries.shape[0]
    local_kv = key_cache.shape[2] // HD
    rep = H // KVH
    pool = key_cache.shape[0]
    page_len = key_cache.shape[1]
    max_pages = page_table.shape[1]
    query = queries.reshape(rows, local_kv, rep, HD)
    pre_q = query[:PRE_DEV]
    dec_q = query[PRE_DEV:]
    start = stretch_start[0]

    pre_keys = key_cache[page_table[0]].reshape(max_pages * page_len, local_kv, HD)
    pre_vals = value_cache[page_table[0]].reshape(max_pages * page_len, local_kv, HD)
    position = jnp.arange(max_pages * page_len, dtype=jnp.int32)
    limit = start + jnp.arange(PRE_DEV, dtype=jnp.int32) + 1
    pre_scores = jnp.einsum(
        "rghd,tgd->rght", pre_q, pre_keys, preferred_element_type=jnp.float32
    )
    pre_weight = capped_weight(
        pre_scores, position[None, None, None, :] < limit[:, None, None, None]
    )
    pre_num = jnp.einsum(
        "rght,tgd->rghd",
        pre_weight.astype(jnp.bfloat16),
        pre_vals,
        preferred_element_type=jnp.float32,
    )
    pre_den = jnp.sum(pre_weight, axis=-1)

    table = page_table[1:]
    page_idx = jnp.arange(max_pages, dtype=jnp.int32)
    used = page_idx[None, :] * page_len < decode_len[:, None]
    owned = (table[:, :, None] == jnp.arange(pool, dtype=jnp.int32)[None, None, :]) & used[
        :, :, None
    ]
    base = jnp.min(
        jnp.where(owned, page_idx[None, :, None] * page_len, jnp.int32(1 << 30)), axis=1
    )
    dec_pos = (base[:, :, None] + jnp.arange(page_len, dtype=jnp.int32)[None, None, :]).reshape(
        DEC_DEV, pool * page_len
    )
    all_keys = key_cache.reshape(pool * page_len, local_kv, HD)
    all_vals = value_cache.reshape(pool * page_len, local_kv, HD)
    dec_scores = jnp.einsum(
        "rghd,tgd->rght", dec_q, all_keys, preferred_element_type=jnp.float32
    )
    dec_weight = capped_weight(dec_scores, (dec_pos < decode_len[:, None])[:, None, None, :])
    dec_num = jnp.einsum(
        "rght,tgd->rghd",
        dec_weight.astype(jnp.bfloat16),
        all_vals,
        preferred_element_type=jnp.float32,
    )
    dec_den = jnp.sum(dec_weight, axis=-1)

    pre_out = (pre_num / pre_den[..., None]).astype(jnp.bfloat16)
    dec_out = (dec_num / dec_den[..., None]).astype(jnp.bfloat16)
    return jnp.concatenate([pre_out, dec_out], axis=0).reshape(rows, local_kv * rep * HD)


def ring_sum(partial, axis):
    count = lax.axis_size(axis)
    me = lax.axis_index(axis)
    rows = partial.shape[0] // count
    chunks = partial.reshape(count, rows, partial.shape[1])
    total = jnp.take(chunks, me, axis=0).astype(jnp.float32)
    for shift in range(1, count):
        sent = jnp.take(chunks, (me + shift) % count, axis=0)
        pairs = [(j, (j + shift) % count) for j in range(count)]
        total = total + lax.ppermute(sent, axis, pairs).astype(jnp.float32)
    reduced = total.astype(jnp.bfloat16)
    pieces = [reduced]
    for shift in range(1, count):
        pairs = [(j, (j + shift) % count) for j in range(count)]
        pieces.append(lax.ppermute(reduced, axis, pairs))
    order = (me - jnp.arange(count, dtype=jnp.int32)) % count
    return jnp.take(jnp.stack(pieces), order, axis=0).reshape(partial.shape)


def per_device(
    queries,
    key_cache,
    value_cache,
    decode_len,
    stretch_start,
    page_table,
    hidden_in,
    o_weight,
    attn_gain,
    ffn_in_gain,
    ffn_out_gain,
    w_gate,
    w_up,
    w_down,
):
    weights = lax.all_gather(
        jnp.stack([w_gate, w_up, w_down]), "req", axis=1, tiled=True
    )
    attended = attend(queries, key_cache, value_cache, decode_len, stretch_start, page_table)
    projected = ring_sum(
        jnp.dot(attended, o_weight, preferred_element_type=jnp.float32).astype(jnp.bfloat16), "mlp"
    ).astype(jnp.float32)
    resid = hidden_in.astype(jnp.float32) + rms(projected, attn_gain)
    normed = rms(resid, ffn_in_gain).astype(jnp.bfloat16)
    gate = jnp.dot(normed, weights[0], preferred_element_type=jnp.float32)
    up_part = jnp.dot(normed, weights[1], preferred_element_type=jnp.float32)
    act = (jax.nn.gelu(gate, approximate=True) * up_part).astype(jnp.bfloat16)
    partial_out = lax.dot_general(
        act, weights[2], (((1,), (1,)), ((), ())), preferred_element_type=jnp.float32
    )
    total = lax.psum_scatter(
        partial_out.astype(jnp.bfloat16), "mlp", scatter_dimension=1, tiled=True
    ).astype(jnp.float32)
    width = total.shape[1]
    first = lax.axis_index("mlp") * width
    square = lax.psum(jnp.sum(total * total, axis=-1, keepdims=True), "mlp")
    scale = lax.rsqrt(square / hidden_in.shape[1] + EPS)
    gain = lax.dynamic_slice_in_dim(ffn_out_gain, first, width, 0)
    kept = lax.dynamic_slice_in_dim(resid, first, width, 1)
    return (kept + total * scale * gain).astype(jnp.bfloat16)


def solution(mesh):
    return jax.shard_map(
        per_device,
        mesh=mesh,
        in_specs=(
            P("req", "mlp"),
            P("req", None, "mlp"),
            P("req", None, "mlp"),
            P("req"),
            P("req"),
            P("req", None),
            P("req", None),
            P("mlp", None),
            P(),
            P(),
            P(),
            P("req", "mlp"),
            P("req", "mlp"),
            P("req", "mlp"),
        ),
        out_specs=P("req", "mlp"),
        check_vma=False,
    )
```

```python
import jax
import jax.numpy as jnp
from jax import lax
from jax.sharding import PartitionSpec as P


H = 8
KVH = 4
HD = 256
PRE_DEV = 512
DEC_DEV = 16


EPS = 1e-06
CAP = 50.0


def rms(values, gain):
    return values * lax.rsqrt(jnp.mean(values * values, axis=-1, keepdims=True) + EPS) * gain


def capped_weight(scores, visible):
    capped = CAP * jnp.tanh(scores / (16.0 * CAP))
    return jnp.where(visible, jnp.exp(capped), jnp.float32(0.0))


def attend(queries, key_cache, value_cache, decode_len, stretch_start, page_table):
    rows = queries.shape[0]
    local_kv = key_cache.shape[2] // HD
    rep = H // KVH
    pool = key_cache.shape[0]
    page_len = key_cache.shape[1]
    max_pages = page_table.shape[1]
    query = queries.reshape(rows, local_kv, rep, HD)
    pre_q = query[:PRE_DEV]
    dec_q = query[PRE_DEV:]
    start = stretch_start[0]

    pre_keys = key_cache[page_table[0]].reshape(max_pages * page_len, local_kv, HD)
    pre_vals = value_cache[page_table[0]].reshape(max_pages * page_len, local_kv, HD)
    position = jnp.arange(max_pages * page_len, dtype=jnp.int32)
    limit = start + jnp.arange(PRE_DEV, dtype=jnp.int32) + 1
    pre_scores = jnp.einsum(
        "rghd,tgd->rght", pre_q, pre_keys, preferred_element_type=jnp.float32
    )
    pre_weight = capped_weight(
        pre_scores, position[None, None, None, :] < limit[:, None, None, None]
    )
    pre_num = jnp.einsum(
        "rght,tgd->rghd",
        pre_weight.astype(jnp.bfloat16),
        pre_vals,
        preferred_element_type=jnp.float32,
    )
    pre_den = jnp.sum(pre_weight, axis=-1)

    table = page_table[1:]
    page_idx = jnp.arange(max_pages, dtype=jnp.int32)
    used = page_idx[None, :] * page_len < decode_len[:, None]
    owned = (table[:, :, None] == jnp.arange(pool, dtype=jnp.int32)[None, None, :]) & used[
        :, :, None
    ]
    base = jnp.min(
        jnp.where(owned, page_idx[None, :, None] * page_len, jnp.int32(1 << 30)), axis=1
    )
    dec_pos = (base[:, :, None] + jnp.arange(page_len, dtype=jnp.int32)[None, None, :]).reshape(
        DEC_DEV, pool * page_len
    )
    all_keys = key_cache.reshape(pool * page_len, local_kv, HD)
    all_vals = value_cache.reshape(pool * page_len, local_kv, HD)
    dec_scores = jnp.einsum(
        "rghd,tgd->rght", dec_q, all_keys, preferred_element_type=jnp.float32
    )
    dec_weight = capped_weight(dec_scores, (dec_pos < decode_len[:, None])[:, None, None, :])
    dec_num = jnp.einsum(
        "rght,tgd->rghd",
        dec_weight.astype(jnp.bfloat16),
        all_vals,
        preferred_element_type=jnp.float32,
    )
    dec_den = jnp.sum(dec_weight, axis=-1)

    pre_out = (pre_num / pre_den[..., None]).astype(jnp.bfloat16)
    dec_out = (dec_num / dec_den[..., None]).astype(jnp.bfloat16)
    return jnp.concatenate([pre_out, dec_out], axis=0).reshape(rows, local_kv * rep * HD)


def ring_sum(partial, axis):
    count = lax.axis_size(axis)
    me = lax.axis_index(axis)
    rows = partial.shape[0] // count
    chunks = partial.reshape(count, rows, partial.shape[1])
    total = jnp.take(chunks, me, axis=0).astype(jnp.float32)
    for shift in range(1, count):
        sent = jnp.take(chunks, (me + shift) % count, axis=0)
        pairs = [(j, (j + shift) % count) for j in range(count)]
        total = total + lax.ppermute(sent, axis, pairs).astype(jnp.float32)
    reduced = total.astype(jnp.bfloat16)
    pieces = [reduced]
    for shift in range(1, count):
        pairs = [(j, (j + shift) % count) for j in range(count)]
        pieces.append(lax.ppermute(reduced, axis, pairs))
    order = (me - jnp.arange(count, dtype=jnp.int32)) % count
    return jnp.take(jnp.stack(pieces), order, axis=0).reshape(partial.shape)


def ring_scatter(partial, axis):
    count = lax.axis_size(axis)
    me = lax.axis_index(axis)
    width = partial.shape[1] // count
    total = lax.dynamic_slice_in_dim(partial, me * width, width, 1).astype(jnp.float32)
    for shift in range(1, count):
        sent = lax.dynamic_slice_in_dim(partial, ((me + shift) % count) * width, width, 1)
        pairs = [(j, (j + shift) % count) for j in range(count)]
        total = total + lax.ppermute(sent, axis, pairs).astype(jnp.float32)
    return total


def per_device(
    queries,
    key_cache,
    value_cache,
    decode_len,
    stretch_start,
    page_table,
    hidden_in,
    o_weight,
    attn_gain,
    ffn_in_gain,
    ffn_out_gain,
    w_gate,
    w_up,
    w_down,
):
    weights = lax.all_gather(
        jnp.stack([w_gate, w_up, w_down]), "req", axis=1, tiled=True
    )
    attended = attend(queries, key_cache, value_cache, decode_len, stretch_start, page_table)
    projected = ring_sum(
        jnp.dot(attended, o_weight, preferred_element_type=jnp.float32).astype(jnp.bfloat16), "mlp"
    ).astype(jnp.float32)
    resid = hidden_in.astype(jnp.float32) + rms(projected, attn_gain)
    normed = rms(resid, ffn_in_gain).astype(jnp.bfloat16)
    gate = jnp.dot(normed, weights[0], preferred_element_type=jnp.float32)
    up_part = jnp.dot(normed, weights[1], preferred_element_type=jnp.float32)
    act = (jax.nn.gelu(gate, approximate=True) * up_part).astype(jnp.bfloat16)
    partial_out = lax.dot_general(
        act, weights[2], (((1,), (1,)), ((), ())), preferred_element_type=jnp.float32
    )
    total = ring_scatter(partial_out.astype(jnp.bfloat16), "mlp")
    width = total.shape[1]
    first = lax.axis_index("mlp") * width
    square = lax.psum(jnp.sum(total * total, axis=-1, keepdims=True), "mlp")
    scale = lax.rsqrt(square / hidden_in.shape[1] + EPS)
    gain = lax.dynamic_slice_in_dim(ffn_out_gain, first, width, 0)
    kept = lax.dynamic_slice_in_dim(resid, first, width, 1)
    return (kept + total * scale * gain).astype(jnp.bfloat16)


def solution(mesh):
    return jax.shard_map(
        per_device,
        mesh=mesh,
        in_specs=(
            P("req", "mlp"),
            P("req", None, "mlp"),
            P("req", None, "mlp"),
            P("req"),
            P("req"),
            P("req", None),
            P("req", None),
            P("mlp", None),
            P(),
            P(),
            P(),
            P("req", "mlp"),
            P("req", "mlp"),
            P("req", "mlp"),
        ),
        out_specs=P("req", "mlp"),
        check_vma=False,
    )
```

```python
import jax
import jax.numpy as jnp
from jax import lax
from jax.sharding import PartitionSpec as P


H = 8
KVH = 4
HD = 256
PRE_DEV = 512
DEC_DEV = 16


EPS = 1e-06
CAP = 50.0


def rms(values, gain):
    return values * lax.rsqrt(jnp.mean(values * values, axis=-1, keepdims=True) + EPS) * gain


def capped_weight(scores, visible):
    capped = CAP * jnp.tanh(scores / (16.0 * CAP))
    return jnp.where(visible, jnp.exp(capped), jnp.float32(0.0))


def attend(queries, key_cache, value_cache, decode_len, stretch_start, page_table):
    rows = queries.shape[0]
    local_kv = key_cache.shape[2] // HD
    rep = H // KVH
    pool = key_cache.shape[0]
    page_len = key_cache.shape[1]
    max_pages = page_table.shape[1]
    query = queries.reshape(rows, local_kv, rep, HD)
    pre_q = query[:PRE_DEV]
    dec_q = query[PRE_DEV:]
    start = stretch_start[0]

    pre_keys = key_cache[page_table[0]].reshape(max_pages * page_len, local_kv, HD)
    pre_vals = value_cache[page_table[0]].reshape(max_pages * page_len, local_kv, HD)
    position = jnp.arange(max_pages * page_len, dtype=jnp.int32)
    limit = start + jnp.arange(PRE_DEV, dtype=jnp.int32) + 1
    pre_scores = jnp.einsum(
        "rghd,tgd->rght", pre_q, pre_keys, preferred_element_type=jnp.float32
    )
    pre_weight = capped_weight(
        pre_scores, position[None, None, None, :] < limit[:, None, None, None]
    )
    pre_num = jnp.einsum(
        "rght,tgd->rghd",
        pre_weight.astype(jnp.bfloat16),
        pre_vals,
        preferred_element_type=jnp.float32,
    )
    pre_den = jnp.sum(pre_weight, axis=-1)

    table = page_table[1:]
    page_idx = jnp.arange(max_pages, dtype=jnp.int32)
    used = page_idx[None, :] * page_len < decode_len[:, None]
    owned = (table[:, :, None] == jnp.arange(pool, dtype=jnp.int32)[None, None, :]) & used[
        :, :, None
    ]
    base = jnp.min(
        jnp.where(owned, page_idx[None, :, None] * page_len, jnp.int32(1 << 30)), axis=1
    )
    dec_pos = (base[:, :, None] + jnp.arange(page_len, dtype=jnp.int32)[None, None, :]).reshape(
        DEC_DEV, pool * page_len
    )
    all_keys = key_cache.reshape(pool * page_len, local_kv, HD)
    all_vals = value_cache.reshape(pool * page_len, local_kv, HD)
    dec_scores = jnp.einsum(
        "rghd,tgd->rght", dec_q, all_keys, preferred_element_type=jnp.float32
    )
    dec_weight = capped_weight(dec_scores, (dec_pos < decode_len[:, None])[:, None, None, :])
    dec_num = jnp.einsum(
        "rght,tgd->rghd",
        dec_weight.astype(jnp.bfloat16),
        all_vals,
        preferred_element_type=jnp.float32,
    )
    dec_den = jnp.sum(dec_weight, axis=-1)

    pre_out = (pre_num / pre_den[..., None]).astype(jnp.bfloat16)
    dec_out = (dec_num / dec_den[..., None]).astype(jnp.bfloat16)
    return jnp.concatenate([pre_out, dec_out], axis=0).reshape(rows, local_kv * rep * HD)


def ring_sum(partial, axis):
    count = lax.axis_size(axis)
    me = lax.axis_index(axis)
    rows = partial.shape[0] // count
    chunks = partial.reshape(count, rows, partial.shape[1])
    total = jnp.take(chunks, me, axis=0).astype(jnp.float32)
    for shift in range(1, count):
        sent = jnp.take(chunks, (me + shift) % count, axis=0)
        pairs = [(j, (j + shift) % count) for j in range(count)]
        total = total + lax.ppermute(sent, axis, pairs).astype(jnp.float32)
    reduced = total.astype(jnp.bfloat16)
    pieces = [reduced]
    for shift in range(1, count):
        pairs = [(j, (j + shift) % count) for j in range(count)]
        pieces.append(lax.ppermute(reduced, axis, pairs))
    order = (me - jnp.arange(count, dtype=jnp.int32)) % count
    return jnp.take(jnp.stack(pieces), order, axis=0).reshape(partial.shape)


def ring_scatter(partial, axis):
    count = lax.axis_size(axis)
    me = lax.axis_index(axis)
    width = partial.shape[1] // count
    total = lax.dynamic_slice_in_dim(partial, me * width, width, 1).astype(jnp.float32)
    for shift in range(1, count):
        sent = lax.dynamic_slice_in_dim(partial, ((me + shift) % count) * width, width, 1)
        pairs = [(j, (j + shift) % count) for j in range(count)]
        total = total + lax.ppermute(sent, axis, pairs).astype(jnp.float32)
    return total


def ring_total(value, axis):
    count = lax.axis_size(axis)
    total = value
    for shift in range(1, count):
        pairs = [(j, (j + shift) % count) for j in range(count)]
        total = total + lax.ppermute(value, axis, pairs)
    return total


def per_device(
    queries,
    key_cache,
    value_cache,
    decode_len,
    stretch_start,
    page_table,
    hidden_in,
    o_weight,
    attn_gain,
    ffn_in_gain,
    ffn_out_gain,
    w_gate,
    w_up,
    w_down,
):
    weights = lax.all_gather(
        jnp.stack([w_gate, w_up, w_down]), "req", axis=1, tiled=True
    )
    attended = attend(queries, key_cache, value_cache, decode_len, stretch_start, page_table)
    projected = ring_sum(
        jnp.dot(attended, o_weight, preferred_element_type=jnp.float32).astype(jnp.bfloat16), "mlp"
    ).astype(jnp.float32)
    resid = hidden_in.astype(jnp.float32) + rms(projected, attn_gain)
    normed = rms(resid, ffn_in_gain).astype(jnp.bfloat16)
    gate = jnp.dot(normed, weights[0], preferred_element_type=jnp.float32)
    up_part = jnp.dot(normed, weights[1], preferred_element_type=jnp.float32)
    act = (jax.nn.gelu(gate, approximate=True) * up_part).astype(jnp.bfloat16)
    partial_out = lax.dot_general(
        act, weights[2], (((1,), (1,)), ((), ())), preferred_element_type=jnp.float32
    )
    total = ring_scatter(partial_out.astype(jnp.bfloat16), "mlp")
    width = total.shape[1]
    first = lax.axis_index("mlp") * width
    square = ring_total(jnp.sum(total * total, axis=-1), "mlp")[:, None]
    scale = lax.rsqrt(square / hidden_in.shape[1] + EPS)
    gain = lax.dynamic_slice_in_dim(ffn_out_gain, first, width, 0)
    kept = lax.dynamic_slice_in_dim(resid, first, width, 1)
    return (kept + total * scale * gain).astype(jnp.bfloat16)


def solution(mesh):
    return jax.shard_map(
        per_device,
        mesh=mesh,
        in_specs=(
            P("req", "mlp"),
            P("req", None, "mlp"),
            P("req", None, "mlp"),
            P("req"),
            P("req"),
            P("req", None),
            P("req", None),
            P("mlp", None),
            P(),
            P(),
            P(),
            P("req", "mlp"),
            P("req", "mlp"),
            P("req", "mlp"),
        ),
        out_specs=P("req", "mlp"),
        check_vma=False,
    )
```

```python
import jax
import jax.numpy as jnp
from jax import lax
from jax.sharding import PartitionSpec as P


H = 8
KVH = 4
HD = 256
PRE_DEV = 512
DEC_DEV = 16


EPS = 1e-06
CAP = 50.0


def rms(values, gain):
    return values * lax.rsqrt(jnp.mean(values * values, axis=-1, keepdims=True) + EPS) * gain


def capped_weight(scores, visible):
    capped = CAP * jnp.tanh(scores / (16.0 * CAP))
    return jnp.where(visible, jnp.exp(capped), jnp.float32(0.0))


def attend(queries, key_cache, value_cache, decode_len, stretch_start, page_table):
    rows = queries.shape[0]
    local_kv = key_cache.shape[2] // HD
    rep = H // KVH
    pool = key_cache.shape[0]
    page_len = key_cache.shape[1]
    max_pages = page_table.shape[1]
    query = queries.reshape(rows, local_kv, rep, HD)
    pre_q = query[:PRE_DEV]
    dec_q = query[PRE_DEV:]
    start = stretch_start[0]

    pre_keys = key_cache[page_table[0]].reshape(max_pages * page_len, local_kv, HD)
    pre_vals = value_cache[page_table[0]].reshape(max_pages * page_len, local_kv, HD)
    position = jnp.arange(max_pages * page_len, dtype=jnp.int32)
    limit = start + jnp.arange(PRE_DEV, dtype=jnp.int32) + 1
    pre_scores = jnp.einsum(
        "rghd,tgd->rght", pre_q, pre_keys, preferred_element_type=jnp.float32
    )
    pre_weight = capped_weight(
        pre_scores, position[None, None, None, :] < limit[:, None, None, None]
    )
    pre_num = jnp.einsum(
        "rght,tgd->rghd",
        pre_weight.astype(jnp.bfloat16),
        pre_vals,
        preferred_element_type=jnp.float32,
    )
    pre_den = jnp.sum(pre_weight, axis=-1)

    table = page_table[1:]
    page_idx = jnp.arange(max_pages, dtype=jnp.int32)
    used = page_idx[None, :] * page_len < decode_len[:, None]
    owned = (table[:, :, None] == jnp.arange(pool, dtype=jnp.int32)[None, None, :]) & used[
        :, :, None
    ]
    base = jnp.min(
        jnp.where(owned, page_idx[None, :, None] * page_len, jnp.int32(1 << 30)), axis=1
    )
    dec_pos = (base[:, :, None] + jnp.arange(page_len, dtype=jnp.int32)[None, None, :]).reshape(
        DEC_DEV, pool * page_len
    )
    all_keys = key_cache.reshape(pool * page_len, local_kv, HD)
    all_vals = value_cache.reshape(pool * page_len, local_kv, HD)
    dec_scores = jnp.einsum(
        "rghd,tgd->rght", dec_q, all_keys, preferred_element_type=jnp.float32
    )
    dec_weight = capped_weight(dec_scores, (dec_pos < decode_len[:, None])[:, None, None, :])
    dec_num = jnp.einsum(
        "rght,tgd->rghd",
        dec_weight.astype(jnp.bfloat16),
        all_vals,
        preferred_element_type=jnp.float32,
    )
    dec_den = jnp.sum(dec_weight, axis=-1)

    pre_out = (pre_num / pre_den[..., None]).astype(jnp.bfloat16)
    dec_out = (dec_num / dec_den[..., None]).astype(jnp.bfloat16)
    return jnp.concatenate([pre_out, dec_out], axis=0).reshape(rows, local_kv * rep * HD)


def ring_sum(partial, axis):
    count = lax.axis_size(axis)
    me = lax.axis_index(axis)
    rows = partial.shape[0] // count
    chunks = partial.reshape(count, rows, partial.shape[1])
    total = jnp.take(chunks, me, axis=0).astype(jnp.float32)
    for shift in range(1, count):
        sent = jnp.take(chunks, (me + shift) % count, axis=0)
        pairs = [(j, (j + shift) % count) for j in range(count)]
        total = total + lax.ppermute(sent, axis, pairs).astype(jnp.float32)
    reduced = total.astype(jnp.bfloat16)
    pieces = [reduced]
    for shift in range(1, count):
        pairs = [(j, (j + shift) % count) for j in range(count)]
        pieces.append(lax.ppermute(reduced, axis, pairs))
    order = (me - jnp.arange(count, dtype=jnp.int32)) % count
    return jnp.take(jnp.stack(pieces), order, axis=0).reshape(partial.shape)


def ring_total(value, axis):
    count = lax.axis_size(axis)
    total = value
    for shift in range(1, count):
        pairs = [(j, (j + shift) % count) for j in range(count)]
        total = total + lax.ppermute(value, axis, pairs)
    return total


def down_scatter(act, down, axis):
    count = lax.axis_size(axis)
    me = lax.axis_index(axis)
    width = down.shape[0] // count

    def block(index):
        rows = lax.dynamic_slice_in_dim(down, index * width, width, 0)
        return lax.dot_general(
            act, rows, (((1,), (1,)), ((), ())), preferred_element_type=jnp.float32
        )

    total = None
    for shift in range(1, count):
        sent = block((me + shift) % count).astype(jnp.bfloat16)
        pairs = [(j, (j + shift) % count) for j in range(count)]
        received = lax.ppermute(sent, axis, pairs).astype(jnp.float32)
        total = received if total is None else total + received
    return total + block(me).astype(jnp.bfloat16).astype(jnp.float32)


def per_device(
    queries,
    key_cache,
    value_cache,
    decode_len,
    stretch_start,
    page_table,
    hidden_in,
    o_weight,
    attn_gain,
    ffn_in_gain,
    ffn_out_gain,
    w_gate,
    w_up,
    w_down,
):
    weights = lax.all_gather(
        jnp.stack([w_gate, w_up, w_down]), "req", axis=1, tiled=True
    )
    attended = attend(queries, key_cache, value_cache, decode_len, stretch_start, page_table)
    projected = ring_sum(
        jnp.dot(attended, o_weight, preferred_element_type=jnp.float32).astype(jnp.bfloat16), "mlp"
    ).astype(jnp.float32)
    resid = hidden_in.astype(jnp.float32) + rms(projected, attn_gain)
    normed = rms(resid, ffn_in_gain).astype(jnp.bfloat16)
    gate = jnp.dot(normed, weights[0], preferred_element_type=jnp.float32)
    up_part = jnp.dot(normed, weights[1], preferred_element_type=jnp.float32)
    act = (jax.nn.gelu(gate, approximate=True) * up_part).astype(jnp.bfloat16)
    act = lax.optimization_barrier(act)
    total = down_scatter(act, weights[2], "mlp")
    width = total.shape[1]
    first = lax.axis_index("mlp") * width
    square = ring_total(jnp.sum(total * total, axis=-1), "mlp")[:, None]
    scale = lax.rsqrt(square / hidden_in.shape[1] + EPS)
    gain = lax.dynamic_slice_in_dim(ffn_out_gain, first, width, 0)
    kept = lax.dynamic_slice_in_dim(resid, first, width, 1)
    return (kept + total * scale * gain).astype(jnp.bfloat16)


def solution(mesh):
    return jax.shard_map(
        per_device,
        mesh=mesh,
        in_specs=(
            P("req", "mlp"),
            P("req", None, "mlp"),
            P("req", None, "mlp"),
            P("req"),
            P("req"),
            P("req", None),
            P("req", None),
            P("mlp", None),
            P(),
            P(),
            P(),
            P("req", "mlp"),
            P("req", "mlp"),
            P("req", "mlp"),
        ),
        out_specs=P("req", "mlp"),
        check_vma=False,
    )
```

```python
import jax
import jax.numpy as jnp
from jax import lax
from jax.sharding import PartitionSpec as P


H = 8
KVH = 4
HD = 256
PRE_DEV = 512
DEC_DEV = 16


EPS = 1e-06
CAP = 50.0


def rms(values, gain):
    return values * lax.rsqrt(jnp.mean(values * values, axis=-1, keepdims=True) + EPS) * gain


def capped_weight(scores, visible):
    capped = CAP * jnp.tanh(scores / (16.0 * CAP))
    return jnp.where(visible, jnp.exp(capped), jnp.float32(0.0))


def attend(queries, key_cache, value_cache, decode_len, stretch_start, page_table):
    rows = queries.shape[0]
    local_kv = key_cache.shape[2] // HD
    rep = H // KVH
    pool = key_cache.shape[0]
    page_len = key_cache.shape[1]
    max_pages = page_table.shape[1]
    query = queries.reshape(rows, local_kv, rep, HD)
    pre_q = query[:PRE_DEV]
    dec_q = query[PRE_DEV:]
    start = stretch_start[0]

    pre_keys = key_cache[page_table[0]].reshape(max_pages * page_len, local_kv, HD)
    pre_vals = value_cache[page_table[0]].reshape(max_pages * page_len, local_kv, HD)
    position = jnp.arange(max_pages * page_len, dtype=jnp.int32)
    limit = start + jnp.arange(PRE_DEV, dtype=jnp.int32) + 1
    pre_scores = jnp.einsum(
        "rghd,tgd->rght", pre_q, pre_keys, preferred_element_type=jnp.float32
    )
    pre_weight = capped_weight(
        pre_scores, position[None, None, None, :] < limit[:, None, None, None]
    )
    pre_num = jnp.einsum(
        "rght,tgd->rghd",
        pre_weight.astype(jnp.bfloat16),
        pre_vals,
        preferred_element_type=jnp.float32,
    )
    pre_den = jnp.sum(pre_weight, axis=-1)

    table = page_table[1:]
    page_idx = jnp.arange(max_pages, dtype=jnp.int32)
    used = page_idx[None, :] * page_len < decode_len[:, None]
    owned = (table[:, :, None] == jnp.arange(pool, dtype=jnp.int32)[None, None, :]) & used[
        :, :, None
    ]
    base = jnp.min(
        jnp.where(owned, page_idx[None, :, None] * page_len, jnp.int32(1 << 30)), axis=1
    )
    dec_pos = (base[:, :, None] + jnp.arange(page_len, dtype=jnp.int32)[None, None, :]).reshape(
        DEC_DEV, pool * page_len
    )
    all_keys = key_cache.reshape(pool * page_len, local_kv, HD)
    all_vals = value_cache.reshape(pool * page_len, local_kv, HD)
    dec_scores = jnp.einsum(
        "rghd,tgd->rght", dec_q, all_keys, preferred_element_type=jnp.float32
    )
    dec_weight = capped_weight(dec_scores, (dec_pos < decode_len[:, None])[:, None, None, :])
    dec_num = jnp.einsum(
        "rght,tgd->rghd",
        dec_weight.astype(jnp.bfloat16),
        all_vals,
        preferred_element_type=jnp.float32,
    )
    dec_den = jnp.sum(dec_weight, axis=-1)

    pre_out = (pre_num / pre_den[..., None]).astype(jnp.bfloat16)
    dec_out = (dec_num / dec_den[..., None]).astype(jnp.bfloat16)
    return jnp.concatenate([pre_out, dec_out], axis=0).reshape(rows, local_kv * rep * HD)


def ring_sum(partial, axis):
    count = lax.axis_size(axis)
    me = lax.axis_index(axis)
    rows = partial.shape[0] // count
    chunks = partial.reshape(count, rows, partial.shape[1])
    total = jnp.take(chunks, me, axis=0).astype(jnp.float32)
    for shift in range(1, count):
        sent = jnp.take(chunks, (me + shift) % count, axis=0)
        pairs = [(j, (j + shift) % count) for j in range(count)]
        total = total + lax.ppermute(sent, axis, pairs).astype(jnp.float32)
    reduced = total.astype(jnp.bfloat16)
    pieces = [reduced]
    for shift in range(1, count):
        pairs = [(j, (j + shift) % count) for j in range(count)]
        pieces.append(lax.ppermute(reduced, axis, pairs))
    order = (me - jnp.arange(count, dtype=jnp.int32)) % count
    return jnp.take(jnp.stack(pieces), order, axis=0).reshape(partial.shape)


def ring_total(value, axis):
    count = lax.axis_size(axis)
    total = value
    for shift in range(1, count):
        pairs = [(j, (j + shift) % count) for j in range(count)]
        total = total + lax.ppermute(value, axis, pairs)
    return total


def down_scatter(act, down, axis):
    count = lax.axis_size(axis)
    me = lax.axis_index(axis)
    width = down.shape[1] // count

    def block(index):
        rows = lax.dynamic_slice(down, (2, index * width, 0), (1, width, down.shape[2]))[0]
        return lax.dot_general(
            act, rows, (((1,), (1,)), ((), ())), preferred_element_type=jnp.float32
        )

    total = None
    for shift in range(1, count):
        sent = block((me + shift) % count).astype(jnp.bfloat16)
        pairs = [(j, (j + shift) % count) for j in range(count)]
        received = lax.ppermute(sent, axis, pairs).astype(jnp.float32)
        total = received if total is None else total + received
    return total + block(me).astype(jnp.bfloat16).astype(jnp.float32)


def per_device(
    queries,
    key_cache,
    value_cache,
    decode_len,
    stretch_start,
    page_table,
    hidden_in,
    o_weight,
    attn_gain,
    ffn_in_gain,
    ffn_out_gain,
    w_gate,
    w_up,
    w_down,
):
    weights = lax.all_gather(
        jnp.stack([w_gate, w_up, w_down]), "req", axis=1, tiled=True
    )
    attended = attend(queries, key_cache, value_cache, decode_len, stretch_start, page_table)
    projected = ring_sum(
        jnp.dot(attended, o_weight, preferred_element_type=jnp.float32).astype(jnp.bfloat16), "mlp"
    ).astype(jnp.float32)
    resid = hidden_in.astype(jnp.float32) + rms(projected, attn_gain)
    normed = lax.optimization_barrier(rms(resid, ffn_in_gain).astype(jnp.bfloat16))
    gate = jnp.dot(normed, weights[0], preferred_element_type=jnp.float32)
    up_part = jnp.dot(normed, weights[1], preferred_element_type=jnp.float32)
    act = (jax.nn.gelu(gate, approximate=True) * up_part).astype(jnp.bfloat16)
    act = lax.optimization_barrier(act)
    total = down_scatter(act, weights, "mlp")
    width = total.shape[1]
    first = lax.axis_index("mlp") * width
    square = ring_total(jnp.sum(total * total, axis=-1), "mlp")[:, None]
    scale = lax.rsqrt(square / hidden_in.shape[1] + EPS)
    gain = lax.dynamic_slice_in_dim(ffn_out_gain, first, width, 0)
    kept = lax.dynamic_slice_in_dim(resid, first, width, 1)
    return (kept + total * scale * gain).astype(jnp.bfloat16)


def solution(mesh):
    return jax.shard_map(
        per_device,
        mesh=mesh,
        in_specs=(
            P("req", "mlp"),
            P("req", None, "mlp"),
            P("req", None, "mlp"),
            P("req"),
            P("req"),
            P("req", None),
            P("req", None),
            P("mlp", None),
            P(),
            P(),
            P(),
            P("req", "mlp"),
            P("req", "mlp"),
            P("req", "mlp"),
        ),
        out_specs=P("req", "mlp"),
        check_vma=False,
    )
```
